32 devices in a mesh: grp: 4 (over y, core), blk: 8 (over z, x).
Axes of the slice: x: 2, y: 2, z: 4, core: 2. Of those that a mesh axis runs over, the one named last changes fastest.
Arguments:
- features: bfloat16 [4096, 128], P(('grp', 'blk')), may hold values from -6 to 6
- col_scale: float32 [4096], P(('grp', 'blk')), may hold values from 0.5 to 2
- row_scale: float32 [4096], P(('grp', 'blk')), may hold values from 0.5 to 2
- tiles: bfloat16 [1024, 128, 128], P(('grp', 'blk')), may hold values from 0 to 0.03125
- tile_cols: int32 [1024], P(('grp', 'blk')), may hold values from 0 to 3
- weight: bfloat16 [128, 256], replicated, may hold values from -0.5 to 0.5
- cotangent: bfloat16 [4096, 256], P(('grp', 'blk')), may hold values from -0.1875 to 0.1875
- train_mask: int32 [4096], P(('grp', 'blk')), may hold values 0 or 1
Outputs:
- hidden: bfloat16 [4096, 256], P(('grp', 'blk'))
- weight_grad: float32 [128, 256], replicated
The draws below stay inside these ranges and needn't reach their ends.
All inputs are finite; a program needn't handle non-finite values. No bound on the sum of `train_mask` on one device may be relied on, other than what follows from the above.
Results may differ from the reference program's by a relative error of at most 0.0054.
Values may be sent and summed in bfloat16 or wider, within the bound.
A program may use at most 128 MiB of HBM per device.

```python
import math
import jax
import jax.numpy as jnp
from jax import lax

FIN = 128
HID = 256
TILE = 128
TPR = 4
NODE_DEV = 128
NODES = 4096
COL_BLOCKS = 4
TILES_ALL = 1024
N_GRP = 4
N_BLK = 8


def plant(drawn, own_key, least, largest):
    longest = drawn.shape.index(max(drawn.shape))
    spots = []
    for shift in (0, 1):
        where = [jax.random.randint(jax.random.fold_in(own_key, axis), (), 0, length) for axis, length in enumerate(drawn.shape)]
        where[longest] = (where[longest] + shift) % drawn.shape[longest]
        spots.append(tuple(where))
    return drawn.at[spots[0]].set(least).at[spots[1]].set(largest)


def shard_levels(key, extent, pieces, smallest, largest):
    gain, own = 1.0, jax.random.fold_in(key, 6)
    for dim, blocks in pieces:
        steps = jnp.exp(jax.random.uniform(jax.random.fold_in(own, dim), (blocks,), jnp.float32, smallest / len(pieces), largest / len(pieces)))
        gain = gain * jnp.repeat(steps, extent[dim] // blocks).reshape([-1 if axis == dim else 1 for axis in range(len(extent))])
    return gain


def scatter_about(key, dims, deviation, most, split=(), dtype=jnp.bfloat16):
    array = jax.random.normal(key, dims, jnp.float32) * deviation
    if len(split) > 0:
        array = shard_levels(key, dims, split, -0.22, 0.18) * array
    return jnp.clip(array, min=-most, max=most).astype(dtype)


def setup_inputs(seed: int = 0) -> dict:
    keys = jax.random.split(jax.random.key(seed), 9)
    return {
        "features": scatter_about(keys[0], (NODES, FIN), 1.0, 6.0, ((0, 32),)),
        "col_scale": jnp.clip(jnp.exp(math.log(2.0) - 1.3862944 * jax.random.uniform(keys[1], (NODES,), jnp.float32) ** shard_levels(keys[1], (NODES,), ((0, 32),), -0.2, 0.2)), 0.5, 2.0),
        "row_scale": jnp.clip(jnp.exp(math.log(2.0) - 1.3862944 * jax.random.uniform(keys[2], (NODES,), jnp.float32) ** shard_levels(keys[2], (NODES,), ((0, 32),), -0.2, 0.2)), 0.5, 2.0),
        "tiles": jnp.clip(0.03125 * jax.random.uniform(keys[3], (TILES_ALL, TILE, TILE), jnp.float32) ** shard_levels(keys[3], (TILES_ALL, TILE, TILE), ((0, 32),), -0.2, 0.2), 0.0, 0.03125).astype(jnp.bfloat16),
        "tile_cols": plant(jax.random.randint(keys[4], (TILES_ALL,), 0, COL_BLOCKS), jax.random.fold_in(keys[4], 1), 0, COL_BLOCKS - 1).astype(jnp.int32),
        "weight": scatter_about(keys[5], (FIN, HID), FIN ** -0.5, 0.5),
        "cotangent": scatter_about(keys[6], (NODES, HID), (2 * NODES ** -0.5), 0.1875, ((0, 32),)),
        "train_mask": plant((jax.random.randint(keys[7], (NODES,), 0, 4) < 1).astype(jnp.int32), jax.random.fold_in(keys[7], 1), 0, 1),
    }


def activate(values):
    return jax.nn.gelu(values, approximate=True)

def reference(features, col_scale, row_scale, tiles, tile_cols, weight, cotangent, train_mask):
    per_dev = NODE_DEV // TILE
    scaled = (col_scale[:, None] * features.astype(jnp.float32)).astype(jnp.bfloat16)
    blocks = scaled.reshape(N_GRP, N_BLK, per_dev, TILE, FIN)
    tile_view = tiles.reshape(N_GRP, N_BLK, N_BLK * per_dev * TPR, TILE, TILE)
    col_view = tile_cols.reshape(N_GRP, N_BLK, N_BLK * per_dev * TPR)

    def group(gindex):

        def step(total, bindex):
            source = lax.dynamic_index_in_dim(blocks, bindex, 1, keepdims=False)
            source = source.reshape(N_GRP * per_dev, TILE, FIN)
            picked = source[col_view[gindex, bindex]].astype(jnp.float32)
            picked = picked.reshape(N_BLK * per_dev, TPR, TILE, FIN)
            piece = tile_view[gindex, bindex].astype(jnp.float32).reshape(N_BLK * per_dev, TPR, TILE, TILE)
            return (total + jnp.einsum('rkij,rkjf->rif', piece, picked), None)
        start = jnp.zeros((N_BLK * per_dev, TILE, FIN), jnp.float32)
        total, _ = lax.scan(step, start, jnp.arange(N_BLK))
        return total
    aggregate = lax.map(group, jnp.arange(N_GRP)).reshape(NODES, FIN)
    mixed = row_scale[:, None] * aggregate
    pre = jnp.dot(mixed, weight.astype(jnp.float32), precision=lax.Precision.HIGHEST)
    hidden, backward = jax.vjp(activate, pre)
    masked_grad = cotangent.astype(jnp.float32) * train_mask.astype(jnp.float32)[:, None]
    delta = backward(masked_grad)[0]
    weight_grad = jnp.dot(mixed.T, delta, precision=lax.Precision.HIGHEST)
    return (hidden.astype(jnp.bfloat16), weight_grad)
```

```python
import functools
import math

import jax
import jax.numpy as jnp
from jax import lax
from jax.experimental import pallas as pl
from jax.experimental.pallas import tpu as pltpu
from jax.sharding import PartitionSpec as P

TPR = 4
ROOT = math.sqrt(2.0 / math.pi)
CUBE = 0.044715
MESH = pl.DeviceIdType.MESH
F32 = jnp.float32
BF16 = jnp.bfloat16
GRAD_LINK = F32


def far_first(count):
    return sorted(range(1, count), key=lambda step: abs(2 * step - count))


def split(value):
    high = value.astype(BF16)
    return high, (value - high.astype(F32)).astype(BF16)


def down_rows(row, width):
    return jnp.broadcast_to(row, (width, row.shape[1])).T


def kernel(n_grp, n_blk, pieces, cols, features, col_scale, row_scale, tiles, weight, cotangent,
           train_mask, hidden_out, grad_out, feat, cscale, rscale, mask, wgt, cot, held, sources,
           mine, outgoing, arrived, hid, grad_parts, grad_in, grad_all, in_sems, tile_sems, src_send,
           src_recv, part_send, part_recv, grad_sems, out_sems):
    g, b = lax.axis_index("grp"), lax.axis_index("blk")
    order = far_first(n_blk) + [0]

    def grp_peer(step):
        return lax.rem(g + step, n_grp)

    def blk_peer(step):
        return lax.rem(b + step, n_blk)

    def load(source, target, sem):
        copy = pltpu.make_async_copy(source, target, sem)
        copy.start()
        return copy

    first = [load(features, feat, in_sems.at[0]), load(col_scale, cscale, in_sems.at[1])]

    barrier = pltpu.get_barrier_semaphore()
    for step in range(1, n_grp):
        pl.semaphore_signal(barrier, inc=1, device_id=(grp_peer(step), b), device_id_type=MESH)
    for step in range(1, n_blk):
        pl.semaphore_signal(barrier, inc=1, device_id=(g, blk_peer(step)), device_id_type=MESH)

    tile_loads = []
    for spot, step in enumerate(order):
        rows = pl.ds(blk_peer(step) * TPR, TPR)
        tile_loads.append(load(tiles.at[rows], held.at[rows], tile_sems.at[spot]))
    late = [
        load(row_scale, rscale, in_sems.at[2]),
        load(train_mask, mask, in_sems.at[3]),
        load(weight, wgt, in_sems.at[4]),
        load(cotangent, cot, in_sems.at[5]),
    ]

    for copy in first:
        copy.wait()
    sources[g] = (down_rows(cscale[...], feat.shape[1]) * feat[...].astype(F32)).astype(BF16)
    pl.semaphore_wait(barrier, n_grp + n_blk - 2)

    src_copies = []
    for step in range(1, n_grp):
        copy = pltpu.make_async_remote_copy(
            src_ref=sources.at[g], dst_ref=sources.at[g],
            send_sem=src_send.at[step - 1], recv_sem=src_recv.at[step - 1],
            device_id=(grp_peer(step), b), device_id_type=MESH)
        copy.start()
        src_copies.append(copy)
    for copy in tile_loads:
        copy.wait()
    for copy in src_copies:
        copy.wait()

    def partial(block):
        base = block * TPR
        left = jnp.concatenate([held[base + k] for k in range(TPR)], axis=1)
        right = jnp.concatenate([sources[cols[base + k]] for k in range(TPR)], axis=0)
        return jnp.dot(left, right, preferred_element_type=F32)

    part_copies = []
    for spot, step in enumerate(order[:-1]):
        block = blk_peer(step)
        outgoing[spot] = partial(block).astype(BF16)
        copy = pltpu.make_async_remote_copy(
            src_ref=outgoing.at[spot], dst_ref=arrived.at[spot],
            send_sem=part_send.at[spot], recv_sem=part_recv.at[spot],
            device_id=(g, block), device_id_type=MESH)
        copy.start()
        part_copies.append(copy)
    mine[...] = partial(b)

    for copy in late:
        copy.wait()
    row_full = down_rows(rscale[...], feat.shape[1])
    mask_full = down_rows(mask[...].astype(F32), cot.shape[1] // 2)
    masked = cot[...].astype(F32) * jnp.concatenate([mask_full, mask_full], axis=1)

    total = mine[...]
    for spot, copy in reversed(list(enumerate(part_copies))):
        copy.wait()
        total = total + arrived[spot].astype(F32)
    mixed = row_full * total

    high, low = split(mixed)
    w = wgt[...]
    pre = jnp.dot(jnp.concatenate([high, low], axis=1), jnp.concatenate([w, w], axis=0),
                  preferred_element_type=F32)
    square = pre * pre
    bent = jnp.tanh(ROOT * pre * (1.0 + CUBE * square))
    half = 0.5 * (1.0 + bent)
    hid[...] = (pre * half).astype(BF16)
    out_copy = load(hid, hidden_out, out_sems.at[0])
    slope = half + 0.5 * pre * (1.0 - bent * bent) * (ROOT * (1.0 + 3.0 * CUBE * square))
    delta = slope * masked

    high_t, low_t = split(mixed.T)
    d_high, d_low = split(delta)
    grad = jnp.dot(jnp.concatenate([high_t, low_t, high_t], axis=1),
                   jnp.concatenate([d_high, d_high, d_low], axis=0), preferred_element_type=F32)
    if not pieces:
        grad_all[...] = grad
        load(grad_all, grad_out, out_sems.at[1]).wait()
        out_copy.wait()
        return

    n = n_grp * n_blk
    me = g * n_blk + b
    wide = grad.shape[1] // 128
    for piece in range(n):
        at, lane = piece // wide * 8, piece % wide * 128
        grad_parts[piece] = grad[at:at + 8, lane:lane + 128].astype(GRAD_LINK)

    def scatter(step, _):
        to = lax.rem(me + step, n)
        pltpu.make_async_remote_copy(
            src_ref=grad_parts.at[to], dst_ref=grad_in.at[n - 1 - step],
            send_sem=grad_sems.at[0], recv_sem=grad_sems.at[1],
            device_id=(to // n_blk, lax.rem(to, n_blk)), device_id_type=MESH).start()
        return 0

    lax.fori_loop(1, n, scatter, 0)
    some = grad_parts.at[pl.ds(0, n - 1)]
    pltpu.make_async_copy(grad_in, grad_in, grad_sems.at[1]).wait()
    summed = grad_parts[me].astype(F32) + jnp.sum(grad_in[...].astype(F32), axis=0)
    grad_all[me] = summed.astype(GRAD_LINK)

    def gather(step, _):
        to = lax.rem(me + step, n)
        pltpu.make_async_remote_copy(
            src_ref=grad_all.at[me], dst_ref=grad_all.at[me],
            send_sem=grad_sems.at[2], recv_sem=grad_sems.at[3],
            device_id=(to // n_blk, lax.rem(to, n_blk)), device_id_type=MESH).start()
        return 0

    lax.fori_loop(1, n, gather, 0)
    pltpu.make_async_copy(some, some, grad_sems.at[0]).wait()
    pltpu.make_async_copy(some, some, grad_sems.at[2]).wait()
    pltpu.make_async_copy(some, some, grad_sems.at[3]).wait()
    for piece in range(n):
        at, lane = piece // wide * 8, piece % wide * 128
        grad_out[at:at + 8, lane:lane + 128] = grad_all[piece].astype(F32)
    out_copy.wait()


def shards(n_grp, n_blk, features, col_scale, row_scale, tiles, tile_cols, weight, cotangent, train_mask):
    nodes, fin = features.shape
    hid_width = weight.shape[1]
    tile = tiles.shape[1]
    n = n_grp * n_blk
    pieces = n * 8 * 128 == fin * hid_width
    any_space = pl.BlockSpec(memory_space=pl.ANY)
    vmem = pl.BlockSpec(memory_space=pltpu.VMEM)
    if pieces:
        grad_scratch = [
            pltpu.VMEM((n, 8, 128), GRAD_LINK),
            pltpu.VMEM((n - 1, 8, 128), GRAD_LINK),
            pltpu.VMEM((n, 8, 128), GRAD_LINK),
        ]
    else:
        grad_scratch = [
            pltpu.VMEM((8, 128), F32),
            pltpu.VMEM((8, 128), F32),
            pltpu.VMEM((fin, hid_width), F32),
        ]
    dma = pltpu.SemaphoreType.DMA
    hidden, grad = pl.pallas_call(
        functools.partial(kernel, n_grp, n_blk, pieces),
        out_shape=(jax.ShapeDtypeStruct((nodes, hid_width), BF16),
                   jax.ShapeDtypeStruct((fin, hid_width), F32)),
        in_specs=[pl.BlockSpec(memory_space=pltpu.SMEM)] + [any_space] * 7,
        out_specs=(any_space, vmem if pieces else any_space),
        scratch_shapes=[
            pltpu.VMEM((nodes, fin), BF16),
            pltpu.VMEM((1, nodes), F32),
            pltpu.VMEM((1, nodes), F32),
            pltpu.VMEM((1, nodes), jnp.int32),
            pltpu.VMEM((fin, hid_width), BF16),
            pltpu.VMEM((nodes, hid_width), BF16),
            pltpu.VMEM(tiles.shape, BF16),
            pltpu.VMEM((n_grp, tile, fin), BF16),
            pltpu.VMEM((tile, fin), F32),
            pltpu.VMEM((n_blk - 1, tile, fin), BF16),
            pltpu.VMEM((n_blk - 1, tile, fin), BF16),
            pltpu.VMEM((nodes, hid_width), BF16),
            *grad_scratch,
            dma((6,)), dma((n_blk,)), dma((n_grp - 1,)), dma((n_grp - 1,)),
            dma((n_blk - 1,)), dma((n_blk - 1,)), dma((4,)), dma((2,)),
        ],
        compiler_params=pltpu.CompilerParams(
            collective_id=0, has_side_effects=True, vmem_limit_bytes=48 * 1024 * 1024),
    )(tile_cols, features, col_scale.reshape(1, nodes), row_scale.reshape(1, nodes), tiles, weight,
      cotangent, train_mask.reshape(1, nodes))
    if not pieces:
        grad = lax.psum(grad, ("grp", "blk"))
    return hidden, grad


def solution(mesh):
    in_specs = (
        P(("grp", "blk"), None),
        P(("grp", "blk")),
        P(("grp", "blk")),
        P(("grp", "blk"), None, None),
        P(("grp", "blk")),
        P(),
        P(("grp", "blk"), None),
        P(("grp", "blk")),
    )
    out_specs = (P(("grp", "blk"), None), P())
    body = functools.partial(shards, mesh.shape["grp"], mesh.shape["blk"])
    return jax.shard_map(body, mesh=mesh, in_specs=in_specs, out_specs=out_specs, check_vma=False)
```

```python
import functools
import math

import jax
import jax.numpy as jnp
from jax import lax
from jax.experimental import pallas as pl
from jax.experimental.pallas import tpu as pltpu
from jax.sharding import PartitionSpec as P

TPR = 4
ROOT = math.sqrt(2.0 / math.pi)
CUBE = 0.044715
MESH = pl.DeviceIdType.MESH
F32 = jnp.float32
BF16 = jnp.bfloat16
GRAD_LINK = F32
VLIM = 64 * 1024 * 1024


def far_first(count):
    return sorted(range(1, count), key=lambda step: abs(2 * step - count))


def split(value):
    high = value.astype(BF16)
    return high, (value - high.astype(F32)).astype(BF16)


def down_rows(row, width):
    return jnp.broadcast_to(row, (width, row.shape[1])).T


def finish(pieces, hid, grad, hidden_out, grad_out, flat, sems):
    first = pltpu.make_async_copy(hid, hidden_out, sems.at[0])
    first.start()
    if pieces:
        wide = flat.shape[1] // 128
        for piece in range(grad.shape[0]):
            at, lane = piece // wide * 8, piece % wide * 128
            flat[at:at + 8, lane:lane + 128] = grad[piece].astype(F32)
    else:
        flat[...] = grad[...]
    second = pltpu.make_async_copy(flat, grad_out, sems.at[1])
    second.start()
    first.wait()
    second.wait()


def kernel(n_grp, n_blk, pieces, cols_in, features, col_scale, row_scale, tiles, weight, cotangent,
           train_mask, hid, grad_all, cols, feat, cscale, rscale, mask, wgt, cot, held, sources,
           mine, outgoing, arrived, grad_parts, grad_in, in_sems, tile_sems, src_send,
           src_recv, part_send, part_recv, grad_sems):
    g, b = lax.axis_index("grp"), lax.axis_index("blk")
    order = far_first(n_blk) + [0]

    def grp_peer(step):
        return lax.rem(g + step, n_grp)

    def blk_peer(step):
        return lax.rem(b + step, n_blk)

    def load(source, target, sem):
        copy = pltpu.make_async_copy(source, target, sem)
        copy.start()
        return copy

    first = [load(features, feat, in_sems.at[0]), load(col_scale, cscale, in_sems.at[1])]

    cols_load = load(cols_in, cols, in_sems.at[6])

    barrier = pltpu.get_barrier_semaphore()
    for step in range(1, n_grp):
        pl.semaphore_signal(barrier, inc=1, device_id=(grp_peer(step), b), device_id_type=MESH)
    for step in range(1, n_blk):
        pl.semaphore_signal(barrier, inc=1, device_id=(g, blk_peer(step)), device_id_type=MESH)

    tile_loads = []
    for spot, step in enumerate(order):
        rows = pl.ds(blk_peer(step) * TPR, TPR)
        tile_loads.append(load(tiles.at[rows], held.at[rows], tile_sems.at[spot]))
    late = [
        load(row_scale, rscale, in_sems.at[2]),
        load(train_mask, mask, in_sems.at[3]),
        load(weight, wgt, in_sems.at[4]),
        load(cotangent, cot, in_sems.at[5]),
    ]

    for copy in first:
        copy.wait()
    sources[g] = (down_rows(cscale[...], feat.shape[1]) * feat[...].astype(F32)).astype(BF16)
    pl.semaphore_wait(barrier, n_grp + n_blk - 2)

    src_copies = []
    for step in range(1, n_grp):
        copy = pltpu.make_async_remote_copy(
            src_ref=sources.at[g], dst_ref=sources.at[g],
            send_sem=src_send.at[step - 1], recv_sem=src_recv.at[step - 1],
            device_id=(grp_peer(step), b), device_id_type=MESH)
        copy.start()
        src_copies.append(copy)
    cols_load.wait()
    for copy in tile_loads:
        copy.wait()
    for copy in src_copies:
        copy.wait()

    def partial(block):
        base = block * TPR
        left = jnp.concatenate([held[base + k] for k in range(TPR)], axis=1)
        right = jnp.concatenate([sources[cols[base + k]] for k in range(TPR)], axis=0)
        return jnp.dot(left, right, preferred_element_type=F32)

    part_copies = []
    for spot, step in enumerate(order[:-1]):
        block = blk_peer(step)
        outgoing[spot] = partial(block).astype(BF16)
        copy = pltpu.make_async_remote_copy(
            src_ref=outgoing.at[spot], dst_ref=arrived.at[spot],
            send_sem=part_send.at[spot], recv_sem=part_recv.at[spot],
            device_id=(g, block), device_id_type=MESH)
        copy.start()
        part_copies.append(copy)
    mine[...] = partial(b)

    for copy in late:
        copy.wait()
    row_full = down_rows(rscale[...], feat.shape[1])
    mask_full = down_rows(mask[...].astype(F32), cot.shape[1] // 2)
    masked = cot[...].astype(F32) * jnp.concatenate([mask_full, mask_full], axis=1)

    total = mine[...]
    for spot, copy in reversed(list(enumerate(part_copies))):
        copy.wait()
        total = total + arrived[spot].astype(F32)
    mixed = row_full * total

    high, low = split(mixed)
    w = wgt[...]
    pre = jnp.dot(jnp.concatenate([high, low], axis=1), jnp.concatenate([w, w], axis=0),
                  preferred_element_type=F32)
    square = pre * pre
    bent = jnp.tanh(ROOT * pre * (1.0 + CUBE * square))
    half = 0.5 * (1.0 + bent)
    hid[...] = (pre * half).astype(BF16)
    slope = half + 0.5 * pre * (1.0 - bent * bent) * (ROOT * (1.0 + 3.0 * CUBE * square))
    delta = slope * masked

    high_t, low_t = split(mixed.T)
    d_high, d_low = split(delta)
    grad = jnp.dot(jnp.concatenate([high_t, low_t, high_t], axis=1),
                   jnp.concatenate([d_high, d_high, d_low], axis=0), preferred_element_type=F32)
    if not pieces:
        grad_all[...] = grad
        return

    n = n_grp * n_blk
    me = g * n_blk + b
    wide = grad.shape[1] // 128
    for piece in range(n):
        at, lane = piece // wide * 8, piece % wide * 128
        grad_parts[piece] = grad[at:at + 8, lane:lane + 128].astype(GRAD_LINK)

    def scatter(step, _):
        to = lax.rem(me + step, n)
        pltpu.make_async_remote_copy(
            src_ref=grad_parts.at[to], dst_ref=grad_in.at[n - 1 - step],
            send_sem=grad_sems.at[0], recv_sem=grad_sems.at[1],
            device_id=(to // n_blk, lax.rem(to, n_blk)), device_id_type=MESH).start()
        return 0

    lax.fori_loop(1, n, scatter, 0)
    some = grad_parts.at[pl.ds(0, n - 1)]
    pltpu.make_async_copy(grad_in, grad_in, grad_sems.at[1]).wait()
    summed = grad_parts[me].astype(F32) + jnp.sum(grad_in[...].astype(F32), axis=0)
    grad_all[me] = summed.astype(GRAD_LINK)

    def gather(step, _):
        to = lax.rem(me + step, n)
        pltpu.make_async_remote_copy(
            src_ref=grad_all.at[me], dst_ref=grad_all.at[me],
            send_sem=grad_sems.at[2], recv_sem=grad_sems.at[3],
            device_id=(to // n_blk, lax.rem(to, n_blk)), device_id_type=MESH).start()
        return 0

    lax.fori_loop(1, n, gather, 0)
    pltpu.make_async_copy(some, some, grad_sems.at[0]).wait()
    pltpu.make_async_copy(some, some, grad_sems.at[2]).wait()
    pltpu.make_async_copy(some, some, grad_sems.at[3]).wait()


def shards(n_grp, n_blk, features, col_scale, row_scale, tiles, tile_cols, weight, cotangent, train_mask):
    nodes, fin = features.shape
    hid_width = weight.shape[1]
    tile = tiles.shape[1]
    n = n_grp * n_blk
    pieces = n * 8 * 128 == fin * hid_width
    hbm = pl.BlockSpec(memory_space=pltpu.HBM)
    vmem = pl.BlockSpec(memory_space=pltpu.VMEM)
    if pieces:
        grad_scratch = [pltpu.VMEM((n, 8, 128), GRAD_LINK), pltpu.VMEM((n - 1, 8, 128), GRAD_LINK)]
        grad_shape = jax.ShapeDtypeStruct((n, 8, 128), GRAD_LINK)
    else:
        grad_scratch = [pltpu.VMEM((8, 128), F32), pltpu.VMEM((8, 128), F32)]
        grad_shape = jax.ShapeDtypeStruct((fin, hid_width), F32)
    dma = pltpu.SemaphoreType.DMA
    hidden_shape = jax.ShapeDtypeStruct((nodes, hid_width), BF16)
    hidden, grad = pl.pallas_call(
        functools.partial(kernel, n_grp, n_blk, pieces),
        out_shape=(hidden_shape, grad_shape),
        in_specs=[hbm] * 8,
        out_specs=(vmem, vmem),
        scratch_shapes=[
            pltpu.SMEM(tile_cols.shape, jnp.int32),
            pltpu.VMEM((nodes, fin), BF16),
            pltpu.VMEM((1, nodes), F32),
            pltpu.VMEM((1, nodes), F32),
            pltpu.VMEM((1, nodes), jnp.int32),
            pltpu.VMEM((fin, hid_width), BF16),
            pltpu.VMEM((nodes, hid_width), BF16),
            pltpu.VMEM(tiles.shape, BF16),
            pltpu.VMEM((n_grp, tile, fin), BF16),
            pltpu.VMEM((tile, fin), F32),
            pltpu.VMEM((n_blk - 1, tile, fin), BF16),
            pltpu.VMEM((n_blk - 1, tile, fin), BF16),
            *grad_scratch,
            dma((7,)), dma((n_blk,)), dma((n_grp - 1,)), dma((n_grp - 1,)),
            dma((n_blk - 1,)), dma((n_blk - 1,)), dma((4,)),
        ],
        compiler_params=pltpu.CompilerParams(
            collective_id=0, has_side_effects=True, vmem_limit_bytes=VLIM),
    )(tile_cols, features, col_scale.reshape(1, nodes), row_scale.reshape(1, nodes), tiles, weight,
      cotangent, train_mask.reshape(1, nodes))
    hidden, grad = pl.pallas_call(
        functools.partial(finish, pieces),
        out_shape=(hidden_shape, jax.ShapeDtypeStruct((fin, hid_width), F32)),
        in_specs=[vmem, vmem],
        out_specs=(hbm, hbm),
        scratch_shapes=[pltpu.VMEM((fin, hid_width), F32), dma((2,))],
        compiler_params=pltpu.CompilerParams(vmem_limit_bytes=1024 * 1024),
    )(hidden, grad)
    if not pieces:
        grad = lax.psum(grad, ("grp", "blk"))
    return hidden, grad


def solution(mesh):
    in_specs = (
        P(("grp", "blk"), None),
        P(("grp", "blk")),
        P(("grp", "blk")),
        P(("grp", "blk"), None, None),
        P(("grp", "blk")),
        P(),
        P(("grp", "blk"), None),
        P(("grp", "blk")),
    )
    out_specs = (P(("grp", "blk"), None), P())
    body = functools.partial(shards, mesh.shape["grp"], mesh.shape["blk"])
    return jax.shard_map(body, mesh=mesh, in_specs=in_specs, out_specs=out_specs, check_vma=False)
```

```python
import functools
import math

import jax
import jax.numpy as jnp
from jax import lax
from jax.experimental import pallas as pl
from jax.experimental.pallas import tpu as pltpu
from jax.sharding import PartitionSpec as P

TPR = 4
ROOT = math.sqrt(2.0 / math.pi)
CUBE = 0.044715
MESH = pl.DeviceIdType.MESH
F32 = jnp.float32
BF16 = jnp.bfloat16
GRAD_LINK = BF16
VLIM = 64 * 1024 * 1024


def far_first(count):
    return sorted(range(1, count), key=lambda step: abs(2 * step - count))


def split(value):
    high = value.astype(BF16)
    return high, (value - high.astype(F32)).astype(BF16)


def down_rows(row, width):
    return jnp.broadcast_to(row, (width, row.shape[1])).T


def kernel(n_grp, n_blk, pieces, cols_in, features, col_scale, row_scale, tiles, weight, cotangent,
           train_mask, hidden_out, grad_out, cols, feat, cscale, rscale, mask, wgt, cot, held, sources,
           mine, outgoing, arrived, hid, flat, grad_all, grad_parts, grad_in, in_sems, tile_sems, src_send,
           src_recv, part_send, part_recv, grad_sems, out_sems):
    g, b = lax.axis_index("grp"), lax.axis_index("blk")
    order = far_first(n_blk) + [0]

    def grp_peer(step):
        return lax.rem(g + step, n_grp)

    def blk_peer(step):
        return lax.rem(b + step, n_blk)

    def load(source, target, sem):
        copy = pltpu.make_async_copy(source, target, sem)
        copy.start()
        return copy

    first = [load(features, feat, in_sems.at[0]), load(col_scale, cscale, in_sems.at[1])]

    cols_load = load(cols_in, cols, in_sems.at[6])

    barrier = pltpu.get_barrier_semaphore()
    for step in range(1, n_grp):
        pl.semaphore_signal(barrier, inc=1, device_id=(grp_peer(step), b), device_id_type=MESH)
    for step in range(1, n_blk):
        pl.semaphore_signal(barrier, inc=1, device_id=(g, blk_peer(step)), device_id_type=MESH)

    tile_loads = []
    for spot, step in enumerate(order):
        rows = pl.ds(blk_peer(step) * TPR, TPR)
        tile_loads.append(load(tiles.at[rows], held.at[rows], tile_sems.at[spot]))
    late = [
        load(row_scale, rscale, in_sems.at[2]),
        load(train_mask, mask, in_sems.at[3]),
        load(weight, wgt, in_sems.at[4]),
        load(cotangent, cot, in_sems.at[5]),
    ]

    for copy in first:
        copy.wait()
    sources[g] = (down_rows(cscale[...], feat.shape[1]) * feat[...].astype(F32)).astype(BF16)
    pl.semaphore_wait(barrier, n_grp + n_blk - 2)

    src_copies = []
    for step in range(1, n_grp):
        copy = pltpu.make_async_remote_copy(
            src_ref=sources.at[g], dst_ref=sources.at[g],
            send_sem=src_send.at[step - 1], recv_sem=src_recv.at[step - 1],
            device_id=(grp_peer(step), b), device_id_type=MESH)
        copy.start()
        src_copies.append(copy)
    cols_load.wait()
    for copy in tile_loads:
        copy.wait()
    for copy in src_copies:
        copy.wait()

    def partial(block):
        base = block * TPR
        left = jnp.concatenate([held[base + k] for k in range(TPR)], axis=1)
        right = jnp.concatenate([sources[cols[base + k]] for k in range(TPR)], axis=0)
        return jnp.dot(left, right, preferred_element_type=F32)

    part_copies = []
    for spot, step in enumerate(order[:-1]):
        block = blk_peer(step)
        outgoing[spot] = partial(block).astype(BF16)
        copy = pltpu.make_async_remote_copy(
            src_ref=outgoing.at[spot], dst_ref=arrived.at[spot],
            send_sem=part_send.at[spot], recv_sem=part_recv.at[spot],
            device_id=(g, block), device_id_type=MESH)
        copy.start()
        part_copies.append(copy)
    mine[...] = partial(b)

    for copy in late:
        copy.wait()
    row_full = down_rows(rscale[...], feat.shape[1])
    mask_full = down_rows(mask[...].astype(F32), cot.shape[1] // 2)
    masked = cot[...].astype(F32) * jnp.concatenate([mask_full, mask_full], axis=1)

    total = mine[...]
    for spot, copy in reversed(list(enumerate(part_copies))):
        copy.wait()
        total = total + arrived[spot].astype(F32)
    mixed = row_full * total

    high, low = split(mixed)
    w = wgt[...]
    pre = jnp.dot(jnp.concatenate([high, low], axis=1), jnp.concatenate([w, w], axis=0),
                  preferred_element_type=F32)
    square = pre * pre
    bent = jnp.tanh(ROOT * pre * (1.0 + CUBE * square))
    half = 0.5 * (1.0 + bent)
    hid[...] = pre * half
    hidden_copy = load(hid, hidden_out, out_sems.at[0])
    slope = half + 0.5 * pre * (1.0 - bent * bent) * (ROOT * (1.0 + 3.0 * CUBE * square))
    delta = slope * masked

    high_t, low_t = split(mixed.T)
    d_high, d_low = split(delta)
    grad = jnp.dot(jnp.concatenate([high_t, low_t, high_t], axis=1),
                   jnp.concatenate([d_high, d_high, d_low], axis=0), preferred_element_type=F32)
    if not pieces:
        flat[...] = grad
        load(flat, grad_out, out_sems.at[1]).wait()
        hidden_copy.wait()
        return

    n = n_grp * n_blk
    me = g * n_blk + b
    span, first_blk = n_blk // 2, n_blk // 4
    owners = n_grp * span
    owner = (b >= first_blk) & (b < first_blk + span)
    seat = g * span + (b - first_blk)
    for piece in range(owners):
        grad_parts[piece] = grad[piece * 8:piece * 8 + 8].astype(GRAD_LINK)

    def scatter(step, _):
        to = lax.rem(me + step, owners)
        to_g, to_b = to // span, first_blk + lax.rem(to, span)

        @pl.when(to_g * n_blk + to_b != me)
        def _():
            pltpu.make_async_remote_copy(
                src_ref=grad_parts.at[to], dst_ref=grad_in.at[me],
                send_sem=grad_sems.at[0], recv_sem=grad_sems.at[1],
                device_id=(to_g, to_b), device_id_type=MESH).start()
        return 0

    lax.fori_loop(0, owners, scatter, 0)
    some = grad_parts.at[pl.ds(0, owners - 1)]

    @pl.when(owner)
    def _():
        grad_in[me] = grad_parts[seat]
        others = grad_in.at[pl.ds(0, n - 1)]
        pltpu.make_async_copy(others, others, grad_sems.at[1]).wait()
        grad_all[seat] = jnp.sum(grad_in[...].astype(F32), axis=0).astype(GRAD_LINK)

        def gather(step, _):
            to = lax.rem(me + step, n)
            pltpu.make_async_remote_copy(
                src_ref=grad_all.at[seat], dst_ref=grad_all.at[seat],
                send_sem=grad_sems.at[2], recv_sem=grad_sems.at[3],
                device_id=(to // n_blk, lax.rem(to, n_blk)), device_id_type=MESH).start()
            return 0

        lax.fori_loop(1, n, gather, 0)
        pltpu.make_async_copy(some, some, grad_sems.at[0]).wait()
        pltpu.make_async_copy(some, some, grad_sems.at[3]).wait()
        pltpu.make_async_copy(others, others, grad_sems.at[2]).wait()

    @pl.when(jnp.logical_not(owner))
    def _():
        pltpu.make_async_copy(grad_parts, grad_parts, grad_sems.at[0]).wait()
        pltpu.make_async_copy(grad_parts, grad_parts, grad_sems.at[3]).wait()

    for piece in range(owners):
        flat[piece * 8:piece * 8 + 8] = grad_all[piece]
    load(flat, grad_out, out_sems.at[1]).wait()
    hidden_copy.wait()


def shards(n_grp, n_blk, features, col_scale, row_scale, tiles, tile_cols, weight, cotangent, train_mask):
    nodes, fin = features.shape
    hid_width = weight.shape[1]
    tile = tiles.shape[1]
    n = n_grp * n_blk
    pieces = n_grp * (n_blk // 2) * 8 == fin
    hbm = pl.BlockSpec(memory_space=pltpu.HBM)
    if pieces:
        spare, landing = (fin // 8, 8, hid_width), (n, 8, hid_width)
    else:
        spare = landing = (1, 8, 128)
    grad_type = GRAD_LINK if pieces else F32
    grad_shape = jax.ShapeDtypeStruct((fin, hid_width), grad_type)
    dma = pltpu.SemaphoreType.DMA
    hidden_shape = jax.ShapeDtypeStruct((nodes, hid_width), F32)
    hidden, grad = pl.pallas_call(
        functools.partial(kernel, n_grp, n_blk, pieces),
        out_shape=(hidden_shape, grad_shape),
        in_specs=[hbm] * 8,
        out_specs=(hbm, hbm),
        scratch_shapes=[
            pltpu.SMEM(tile_cols.shape, jnp.int32),
            pltpu.VMEM((nodes, fin), BF16),
            pltpu.VMEM((1, nodes), F32),
            pltpu.VMEM((1, nodes), F32),
            pltpu.VMEM((1, nodes), jnp.int32),
            pltpu.VMEM((fin, hid_width), BF16),
            pltpu.VMEM((nodes, hid_width), BF16),
            pltpu.VMEM(tiles.shape, BF16),
            pltpu.VMEM((n_grp, tile, fin), BF16),
            pltpu.VMEM((tile, fin), F32),
            pltpu.VMEM((n_blk - 1, tile, fin), BF16),
            pltpu.VMEM((n_blk - 1, tile, fin), BF16),
            pltpu.VMEM((nodes, hid_width), F32),
            pltpu.VMEM((fin, hid_width), grad_type),
            pltpu.VMEM(spare, GRAD_LINK),
            pltpu.VMEM(spare, GRAD_LINK),
            pltpu.VMEM(landing, GRAD_LINK),
            dma((7,)), dma((n_blk,)), dma((n_grp - 1,)), dma((n_grp - 1,)),
            dma((n_blk - 1,)), dma((n_blk - 1,)), dma((4,)), dma((2,)),
        ],
        compiler_params=pltpu.CompilerParams(
            collective_id=0, has_side_effects=True, vmem_limit_bytes=VLIM),
    )(tile_cols, features, col_scale.reshape(1, nodes), row_scale.reshape(1, nodes), tiles, weight,
      cotangent, train_mask.reshape(1, nodes))
    if not pieces:
        grad = lax.psum(grad, ("grp", "blk"))
    return hidden.astype(BF16), grad.astype(F32)


def solution(mesh):
    in_specs = (
        P(("grp", "blk"), None),
        P(("grp", "blk")),
        P(("grp", "blk")),
        P(("grp", "blk"), None, None),
        P(("grp", "blk")),
        P(),
        P(("grp", "blk"), None),
        P(("grp", "blk")),
    )
    out_specs = (P(("grp", "blk"), None), P())
    body = functools.partial(shards, mesh.shape["grp"], mesh.shape["blk"])
    return jax.shard_map(body, mesh=mesh, in_specs=in_specs, out_specs=out_specs, check_vma=False)
```

```python
import functools
import math

import jax
import jax.numpy as jnp
from jax import lax
from jax.experimental import pallas as pl
from jax.experimental.pallas import tpu as pltpu
from jax.sharding import PartitionSpec as P

TPR = 4
ROOT = math.sqrt(2.0 / math.pi)
CUBE = 0.044715
MESH = pl.DeviceIdType.MESH
F32 = jnp.float32
BF16 = jnp.bfloat16
GRAD_LINK = BF16
VLIM = 64 * 1024 * 1024


def far_first(count):
    return sorted(range(1, count), key=lambda step: abs(2 * step - count))


def split(value):
    high = value.astype(BF16)
    return high, (value - high.astype(F32)).astype(BF16)


def down_rows(row, width):
    return jnp.broadcast_to(row, (width, row.shape[1])).T


def kernel(n_grp, n_blk, pieces, cols_in, features, col_scale, row_scale, tiles, weight, cotangent,
           train_mask, packed, cols, feat, cscale, rscale, mask, wgt, cot, held, sources,
           mine, outgoing, arrived, hid, flat, grad_all, grad_parts, grad_in, in_sems, tile_sems, src_send,
           src_recv, part_send, part_recv, grad_sems, out_sems):
    g, b = lax.axis_index("grp"), lax.axis_index("blk")
    order = far_first(n_blk) + [0]

    def grp_peer(step):
        return lax.rem(g + step, n_grp)

    def blk_peer(step):
        return lax.rem(b + step, n_blk)

    def load(source, target, sem):
        copy = pltpu.make_async_copy(source, target, sem)
        copy.start()
        return copy

    first = [load(features, feat, in_sems.at[0]), load(col_scale, cscale, in_sems.at[1])]

    cols_load = load(cols_in, cols, in_sems.at[6])

    barrier = pltpu.get_barrier_semaphore()
    for step in range(1, n_grp):
        pl.semaphore_signal(barrier, inc=1, device_id=(grp_peer(step), b), device_id_type=MESH)
    for step in range(1, n_blk):
        pl.semaphore_signal(barrier, inc=1, device_id=(g, blk_peer(step)), device_id_type=MESH)

    tile_loads = []
    for spot, step in enumerate(order):
        rows = pl.ds(blk_peer(step) * TPR, TPR)
        tile_loads.append(load(tiles.at[rows], held.at[rows], tile_sems.at[spot]))
    late = [
        load(row_scale, rscale, in_sems.at[2]),
        load(train_mask, mask, in_sems.at[3]),
        load(weight, wgt, in_sems.at[4]),
        load(cotangent, cot, in_sems.at[5]),
    ]

    for copy in first:
        copy.wait()
    sources[g] = (down_rows(cscale[...], feat.shape[1]) * feat[...].astype(F32)).astype(BF16)
    pl.semaphore_wait(barrier, n_grp + n_blk - 2)

    src_copies = []
    for step in range(1, n_grp):
        copy = pltpu.make_async_remote_copy(
            src_ref=sources.at[g], dst_ref=sources.at[g],
            send_sem=src_send.at[step - 1], recv_sem=src_recv.at[step - 1],
            device_id=(grp_peer(step), b), device_id_type=MESH)
        copy.start()
        src_copies.append(copy)
    cols_load.wait()
    for copy in tile_loads:
        copy.wait()
    for copy in src_copies:
        copy.wait()

    def partial(block):
        base = block * TPR
        left = jnp.concatenate([held[base + k] for k in range(TPR)], axis=1)
        right = jnp.concatenate([sources[cols[base + k]] for k in range(TPR)], axis=0)
        return jnp.dot(left, right, preferred_element_type=F32)

    part_copies = []
    for spot, step in enumerate(order[:-1]):
        block = blk_peer(step)
        outgoing[spot] = partial(block).astype(BF16)
        copy = pltpu.make_async_remote_copy(
            src_ref=outgoing.at[spot], dst_ref=arrived.at[spot],
            send_sem=part_send.at[spot], recv_sem=part_recv.at[spot],
            device_id=(g, block), device_id_type=MESH)
        copy.start()
        part_copies.append(copy)
    mine[...] = partial(b)

    for copy in late:
        copy.wait()
    row_full = down_rows(rscale[...], feat.shape[1])
    mask_full = down_rows(mask[...].astype(F32), cot.shape[1] // 2)
    masked = cot[...].astype(F32) * jnp.concatenate([mask_full, mask_full], axis=1)

    total = mine[...]
    for spot, copy in reversed(list(enumerate(part_copies))):
        copy.wait()
        total = total + arrived[spot].astype(F32)
    mixed = row_full * total

    high, low = split(mixed)
    w = wgt[...]
    pre = jnp.dot(jnp.concatenate([high, low], axis=1), jnp.concatenate([w, w], axis=0),
                  preferred_element_type=F32)
    square = pre * pre
    bent = jnp.tanh(ROOT * pre * (1.0 + CUBE * square))
    half = 0.5 * (1.0 + bent)
    hid[...] = (pre * half).astype(hid.dtype)
    hidden_copy = load(hid, packed.at[pl.ds(0, hid.shape[0])], out_sems.at[0])
    slope = half + 0.5 * pre * (1.0 - bent * bent) * (ROOT * (1.0 + 3.0 * CUBE * square))
    delta = slope * masked

    high_t, low_t = split(mixed.T)
    d_high, d_low = split(delta)
    grad = jnp.dot(jnp.concatenate([high_t, low_t, high_t], axis=1),
                   jnp.concatenate([d_high, d_high, d_low], axis=0), preferred_element_type=F32)
    if not pieces:
        flat[...] = grad
        load(flat, packed.at[pl.ds(hid.shape[0], flat.shape[0])], out_sems.at[1]).wait()
        hidden_copy.wait()
        return

    n = n_grp * n_blk
    me = g * n_blk + b
    span, first_blk = n_blk // 2, n_blk // 4
    owners = n_grp * span
    owner = (b >= first_blk) & (b < first_blk + span)
    seat = g * span + (b - first_blk)
    for piece in range(owners):
        grad_parts[piece] = grad[piece * 8:piece * 8 + 8].astype(GRAD_LINK)

    def scatter(step, _):
        to = lax.rem(me + step, owners)
        to_g, to_b = to // span, first_blk + lax.rem(to, span)

        @pl.when(to_g * n_blk + to_b != me)
        def _():
            pltpu.make_async_remote_copy(
                src_ref=grad_parts.at[to], dst_ref=grad_in.at[me],
                send_sem=grad_sems.at[0], recv_sem=grad_sems.at[1],
                device_id=(to_g, to_b), device_id_type=MESH).start()
        return 0

    lax.fori_loop(0, owners, scatter, 0)
    some = grad_parts.at[pl.ds(0, owners - 1)]

    @pl.when(owner)
    def _():
        grad_in[me] = grad_parts[seat]
        others = grad_in.at[pl.ds(0, n - 1)]
        pltpu.make_async_copy(others, others, grad_sems.at[1]).wait()
        grad_all[seat] = jnp.sum(grad_in[...].astype(F32), axis=0).astype(GRAD_LINK)

        def gather(step, _):
            to = lax.rem(me + step, n)
            pltpu.make_async_remote_copy(
                src_ref=grad_all.at[seat], dst_ref=grad_all.at[seat],
                send_sem=grad_sems.at[2], recv_sem=grad_sems.at[3],
                device_id=(to // n_blk, lax.rem(to, n_blk)), device_id_type=MESH).start()
            return 0

        lax.fori_loop(1, n, gather, 0)
        pltpu.make_async_copy(some, some, grad_sems.at[0]).wait()
        pltpu.make_async_copy(some, some, grad_sems.at[3]).wait()
        pltpu.make_async_copy(others, others, grad_sems.at[2]).wait()

    @pl.when(jnp.logical_not(owner))
    def _():
        pltpu.make_async_copy(grad_parts, grad_parts, grad_sems.at[0]).wait()
        pltpu.make_async_copy(grad_parts, grad_parts, grad_sems.at[3]).wait()

    for piece in range(owners):
        flat[piece * 8:piece * 8 + 8] = grad_all[piece]
    load(flat, packed.at[pl.ds(hid.shape[0], flat.shape[0])], out_sems.at[1]).wait()
    hidden_copy.wait()


def shards(n_grp, n_blk, features, col_scale, row_scale, tiles, tile_cols, weight, cotangent, train_mask):
    nodes, fin = features.shape
    hid_width = weight.shape[1]
    tile = tiles.shape[1]
    n = n_grp * n_blk
    pieces = n_grp * (n_blk // 2) * 8 == fin
    hbm = pl.BlockSpec(memory_space=pltpu.HBM)
    if pieces:
        spare, landing = (fin // 8, 8, hid_width), (n, 8, hid_width)
    else:
        spare = landing = (1, 8, 128)
    out_type = BF16 if pieces else F32
    hbm = pl.BlockSpec(memory_space=pltpu.HBM)
    if pieces:
        spare, landing = (fin // 8, 8, hid_width), (n, 8, hid_width)
    else:
        spare = landing = (1, 8, 128)
    grad_type = GRAD_LINK if pieces else F32
    grad_shape = jax.ShapeDtypeStruct((fin, hid_width), grad_type)
    dma = pltpu.SemaphoreType.DMA
    packed_shape = jax.ShapeDtypeStruct((nodes + fin, hid_width), out_type)
    packed = pl.pallas_call(
        functools.partial(kernel, n_grp, n_blk, pieces),
        out_shape=packed_shape,
        in_specs=[hbm] * 8,
        out_specs=hbm,
        scratch_shapes=[
            pltpu.SMEM(tile_cols.shape, jnp.int32),
            pltpu.VMEM((nodes, fin), BF16),
            pltpu.VMEM((1, nodes), F32),
            pltpu.VMEM((1, nodes), F32),
            pltpu.VMEM((1, nodes), jnp.int32),
            pltpu.VMEM((fin, hid_width), BF16),
            pltpu.VMEM((nodes, hid_width), BF16),
            pltpu.VMEM(tiles.shape, BF16),
            pltpu.VMEM((n_grp, tile, fin), BF16),
            pltpu.VMEM((tile, fin), F32),
            pltpu.VMEM((n_blk - 1, tile, fin), BF16),
            pltpu.VMEM((n_blk - 1, tile, fin), BF16),
            pltpu.VMEM((nodes, hid_width), out_type),
            pltpu.VMEM((fin, hid_width), out_type),
            pltpu.VMEM(spare, GRAD_LINK),
            pltpu.VMEM(spare, GRAD_LINK),
            pltpu.VMEM(landing, GRAD_LINK),
            dma((7,)), dma((n_blk,)), dma((n_grp - 1,)), dma((n_grp - 1,)),
            dma((n_blk - 1,)), dma((n_blk - 1,)), dma((4,)), dma((2,)),
        ],
        compiler_params=pltpu.CompilerParams(
            collective_id=0, has_side_effects=True, vmem_limit_bytes=VLIM),
    )(tile_cols, features, col_scale.reshape(1, nodes), row_scale.reshape(1, nodes), tiles, weight,
      cotangent, train_mask.reshape(1, nodes))
    hidden, grad = packed[:nodes].astype(BF16), packed[nodes:].astype(F32)
    if not pieces:
        grad = lax.psum(grad, ("grp", "blk"))
    return hidden, grad


def solution(mesh):
    in_specs = (
        P(("grp", "blk"), None),
        P(("grp", "blk")),
        P(("grp", "blk")),
        P(("grp", "blk"), None, None),
        P(("grp", "blk")),
        P(),
        P(("grp", "blk"), None),
        P(("grp", "blk")),
    )
    out_specs = (P(("grp", "blk"), None), P())
    body = functools.partial(shards, mesh.shape["grp"], mesh.shape["blk"])
    return jax.shard_map(body, mesh=mesh, in_specs=in_specs, out_specs=out_specs, check_vma=False)
```

```python
import functools
import math

import jax
import jax.numpy as jnp
from jax import lax
from jax.experimental import pallas as pl
from jax.experimental.pallas import tpu as pltpu
from jax.sharding import PartitionSpec as P

TPR = 4
ROOT = math.sqrt(2.0 / math.pi)
CUBE = 0.044715
MESH = pl.DeviceIdType.MESH
F32 = jnp.float32
BF16 = jnp.bfloat16
GRAD_LINK = BF16
VLIM = 64 * 1024 * 1024


def far_first(count):
    return sorted(range(1, count), key=lambda step: abs(2 * step - count))


def split(value):
    high = value.astype(BF16)
    return high, (value - high.astype(F32)).astype(BF16)


def down_rows(row, width):
    return jnp.broadcast_to(row, (width, row.shape[1])).T


def kernel(n_grp, n_blk, pieces, cols_in, features, col_scale, row_scale, tiles, weight, cotangent,
           train_mask, packed, cols, feat, cscale, rscale, mask, wgt, cot, held, sources,
           mine, outgoing, arrived, hid, flat, grad_all, grad_parts, grad_in, in_sems, tile_sems, src_send,
           src_recv, part_send, part_recv, grad_sems, out_sems):
    g, b = lax.axis_index("grp"), lax.axis_index("blk")
    order = far_first(n_blk) + [0]

    def grp_peer(step):
        return lax.rem(g + step, n_grp)

    def blk_peer(step):
        return lax.rem(b + step, n_blk)

    def load(source, target, sem):
        copy = pltpu.make_async_copy(source, target, sem)
        copy.start()
        return copy

    first = [load(features, feat, in_sems.at[0]), load(col_scale, cscale, in_sems.at[1])]

    cols_load = load(cols_in, cols, in_sems.at[6])

    barrier = pltpu.get_barrier_semaphore()
    for step in range(1, n_grp):
        pl.semaphore_signal(barrier, inc=1, device_id=(grp_peer(step), b), device_id_type=MESH)
    for step in range(1, n_blk):
        pl.semaphore_signal(barrier, inc=1, device_id=(g, blk_peer(step)), device_id_type=MESH)

    tile_loads = []
    for spot, step in enumerate(order):
        rows = pl.ds(blk_peer(step) * TPR, TPR)
        tile_loads.append(load(tiles.at[rows], held.at[rows], tile_sems.at[spot]))
    late = [
        load(row_scale, rscale, in_sems.at[2]),
        load(train_mask, mask, in_sems.at[3]),
        load(weight, wgt, in_sems.at[4]),
        load(cotangent, cot, in_sems.at[5]),
    ]

    for copy in first:
        copy.wait()
    sources[g] = (down_rows(cscale[...], feat.shape[1]) * feat[...].astype(F32)).astype(BF16)
    pl.semaphore_wait(barrier, n_grp + n_blk - 2)

    src_copies = []
    for step in range(1, n_grp):
        copy = pltpu.make_async_remote_copy(
            src_ref=sources.at[g], dst_ref=sources.at[g],
            send_sem=src_send.at[step - 1], recv_sem=src_recv.at[step - 1],
            device_id=(grp_peer(step), b), device_id_type=MESH)
        copy.start()
        src_copies.append(copy)
    cols_load.wait()
    for copy in tile_loads:
        copy.wait()
    for copy in src_copies:
        copy.wait()

    def partial(block):
        base = block * TPR
        left = jnp.concatenate([held[base + k] for k in range(TPR)], axis=1)
        right = jnp.concatenate([sources[cols[base + k]] for k in range(TPR)], axis=0)
        return jnp.dot(left, right, preferred_element_type=F32)

    part_copies = []
    for spot, step in enumerate(order[:-1]):
        block = blk_peer(step)
        outgoing[spot] = partial(block).astype(BF16)
        copy = pltpu.make_async_remote_copy(
            src_ref=outgoing.at[spot], dst_ref=arrived.at[spot],
            send_sem=part_send.at[spot], recv_sem=part_recv.at[spot],
            device_id=(g, block), device_id_type=MESH)
        copy.start()
        part_copies.append(copy)
    mine[...] = partial(b)

    for copy in late:
        copy.wait()
    row_full = down_rows(rscale[...], feat.shape[1])
    mask_full = down_rows(mask[...].astype(F32), cot.shape[1] // 2)
    masked = cot[...].astype(F32) * jnp.concatenate([mask_full, mask_full], axis=1)

    total = mine[...]
    for spot, copy in reversed(list(enumerate(part_copies))):
        copy.wait()
        total = total + arrived[spot].astype(F32)
    mixed = row_full * total

    high, low = split(mixed)
    w = wgt[...]
    pre = jnp.dot(jnp.concatenate([high, low], axis=1), jnp.concatenate([w, w], axis=0),
                  preferred_element_type=F32)
    square = pre * pre
    bent = jnp.tanh(ROOT * pre * (1.0 + CUBE * square))
    half = 0.5 * (1.0 + bent)
    hid[...] = (pre * half).astype(hid.dtype)
    hidden_copy = load(hid, packed.at[pl.ds(0, hid.shape[0])], out_sems.at[0])
    slope = half + 0.5 * pre * (1.0 - bent * bent) * (ROOT * (1.0 + 3.0 * CUBE * square))
    delta = slope * masked

    high_t, low_t = split(mixed.T)
    d_high, d_low = split(delta)
    grad = jnp.dot(jnp.concatenate([high_t, low_t, high_t], axis=1),
                   jnp.concatenate([d_high, d_high, d_low], axis=0), preferred_element_type=F32)
    if not pieces:
        flat[...] = grad
        load(flat, packed.at[pl.ds(hid.shape[0], flat.shape[0])], out_sems.at[1]).wait()
        hidden_copy.wait()
        return

    n = n_grp * n_blk
    me = g * n_blk + b
    span, first_blk = n_blk // 2, n_blk // 4
    owners = n_grp * span
    owner = (b >= first_blk) & (b < first_blk + span)
    seat = g * span + (b - first_blk)
    for piece in range(owners):
        grad_parts[piece] = grad[piece * 8:piece * 8 + 8].astype(GRAD_LINK)

    def scatter(step, _):
        to = lax.rem(me + step, owners)
        to_g, to_b = to // span, first_blk + lax.rem(to, span)

        @pl.when(to_g * n_blk + to_b != me)
        def _():
            pltpu.make_async_remote_copy(
                src_ref=grad_parts.at[to], dst_ref=grad_in.at[me],
                send_sem=grad_sems.at[0], recv_sem=grad_sems.at[1],
                device_id=(to_g, to_b), device_id_type=MESH).start()
        return 0

    lax.fori_loop(0, owners, scatter, 0)
    some = grad_parts.at[pl.ds(0, owners - 1)]

    @pl.when(owner)
    def _():
        grad_in[me] = grad_parts[seat]
        others = grad_in.at[pl.ds(0, n - 1)]
        pltpu.make_async_copy(others, others, grad_sems.at[1]).wait()
        grad_all[seat] = jnp.sum(grad_in[...].astype(F32), axis=0).astype(GRAD_LINK)

        def gather(step, _):
            to = lax.rem(me + step, n)
            pltpu.make_async_remote_copy(
                src_ref=grad_all.at[seat], dst_ref=grad_all.at[seat],
                send_sem=grad_sems.at[2], recv_sem=grad_sems.at[3],
                device_id=(to // n_blk, lax.rem(to, n_blk)), device_id_type=MESH).start()
            return 0

        lax.fori_loop(1, n, gather, 0)
        pltpu.make_async_copy(some, some, grad_sems.at[3]).wait()

    @pl.when(jnp.logical_not(owner))
    def _():
        pltpu.make_async_copy(grad_parts, grad_parts, grad_sems.at[3]).wait()

    for piece in range(owners):
        flat[piece * 8:piece * 8 + 8] = grad_all[piece]
    grad_copy = load(flat, packed.at[pl.ds(hid.shape[0], flat.shape[0])], out_sems.at[1])

    @pl.when(owner)
    def _():
        others = grad_in.at[pl.ds(0, n - 1)]
        pltpu.make_async_copy(some, some, grad_sems.at[0]).wait()
        pltpu.make_async_copy(others, others, grad_sems.at[2]).wait()

    @pl.when(jnp.logical_not(owner))
    def _():
        pltpu.make_async_copy(grad_parts, grad_parts, grad_sems.at[0]).wait()

    grad_copy.wait()
    hidden_copy.wait()


def shards(n_grp, n_blk, features, col_scale, row_scale, tiles, tile_cols, weight, cotangent, train_mask):
    nodes, fin = features.shape
    hid_width = weight.shape[1]
    tile = tiles.shape[1]
    n = n_grp * n_blk
    pieces = n_grp * (n_blk // 2) * 8 == fin
    hbm = pl.BlockSpec(memory_space=pltpu.HBM)
    if pieces:
        spare, landing = (fin // 8, 8, hid_width), (n, 8, hid_width)
    else:
        spare = landing = (1, 8, 128)
    out_type = BF16 if pieces else F32
    hbm = pl.BlockSpec(memory_space=pltpu.HBM)
    if pieces:
        spare, landing = (fin // 8, 8, hid_width), (n, 8, hid_width)
    else:
        spare = landing = (1, 8, 128)
    grad_type = GRAD_LINK if pieces else F32
    grad_shape = jax.ShapeDtypeStruct((fin, hid_width), grad_type)
    dma = pltpu.SemaphoreType.DMA
    packed_shape = jax.ShapeDtypeStruct((nodes + fin, hid_width), out_type)
    packed = pl.pallas_call(
        functools.partial(kernel, n_grp, n_blk, pieces),
        out_shape=packed_shape,
        in_specs=[hbm] * 8,
        out_specs=hbm,
        scratch_shapes=[
            pltpu.SMEM(tile_cols.shape, jnp.int32),
            pltpu.VMEM((nodes, fin), BF16),
            pltpu.VMEM((1, nodes), F32),
            pltpu.VMEM((1, nodes), F32),
            pltpu.VMEM((1, nodes), jnp.int32),
            pltpu.VMEM((fin, hid_width), BF16),
            pltpu.VMEM((nodes, hid_width), BF16),
            pltpu.VMEM(tiles.shape, BF16),
            pltpu.VMEM((n_grp, tile, fin), BF16),
            pltpu.VMEM((tile, fin), F32),
            pltpu.VMEM((n_blk - 1, tile, fin), BF16),
            pltpu.VMEM((n_blk - 1, tile, fin), BF16),
            pltpu.VMEM((nodes, hid_width), out_type),
            pltpu.VMEM((fin, hid_width), out_type),
            pltpu.VMEM(spare, GRAD_LINK),
            pltpu.VMEM(spare, GRAD_LINK),
            pltpu.VMEM(landing, GRAD_LINK),
            dma((7,)), dma((n_blk,)), dma((n_grp - 1,)), dma((n_grp - 1,)),
            dma((n_blk - 1,)), dma((n_blk - 1,)), dma((4,)), dma((2,)),
        ],
        compiler_params=pltpu.CompilerParams(
            collective_id=0, has_side_effects=True, vmem_limit_bytes=VLIM),
    )(tile_cols, features, col_scale.reshape(1, nodes), row_scale.reshape(1, nodes), tiles, weight,
      cotangent, train_mask.reshape(1, nodes))
    hidden, grad = packed[:nodes].astype(BF16), packed[nodes:].astype(F32)
    if not pieces:
        grad = lax.psum(grad, ("grp", "blk"))
    return hidden, grad


def solution(mesh):
    in_specs = (
        P(("grp", "blk"), None),
        P(("grp", "blk")),
        P(("grp", "blk")),
        P(("grp", "blk"), None, None),
        P(("grp", "blk")),
        P(),
        P(("grp", "blk"), None),
        P(("grp", "blk")),
    )
    out_specs = (P(("grp", "blk"), None), P())
    body = functools.partial(shards, mesh.shape["grp"], mesh.shape["blk"])
    return jax.shard_map(body, mesh=mesh, in_specs=in_specs, out_specs=out_specs, check_vma=False)
```
